32 devices in a mesh: ctx: 8 (over z, y), dp: 4 (over x, core).
Axes of the slice: x: 2, y: 2, z: 4, core: 2. Of those that a mesh axis runs over, the one named last changes fastest.
Arguments:
- tokens: bfloat16 [4, 4096, 768], P('dp', 'ctx'), may hold values from -6 to 6
- cotangent: bfloat16 [4, 4096, 768], P('dp', 'ctx'), may hold values from -6 to 6
- attn_gain: bfloat16 [768], P('dp'), may hold values from 0.099609375 to 1.8984375
- mlp_gain: bfloat16 [768], P('dp'), may hold values from 0.099609375 to 1.8984375
- w_qkv: bfloat16 [768, 2304], P('dp'), may hold values from -0.21875 to 0.21875
- w_out: bfloat16 [768, 768], P('dp'), may hold values from -6 to 6
- w_in: bfloat16 [768, 2304], P('dp'), may hold values from -0.21875 to 0.21875
- w_mlp_out: bfloat16 [1152, 768], P('dp'), may hold values from -0.1875 to 0.1875
- block_offsets: int32 [4, 8], P('dp', 'ctx'), may hold values from 0 to 3584, as said below
Outputs:
- mixed: bfloat16 [4, 4096, 768], P('dp', 'ctx')
- tokens_grad: float32 [4, 4096, 768], P('dp', 'ctx')
- attn_gain_grad: float32 [768], P('dp')
- mlp_gain_grad: float32 [768], P('dp')
- w_qkv_grad: float32 [768, 2304], P('dp')
- w_out_grad: float32 [768, 768], P('dp')
- w_in_grad: float32 [768, 2304], P('dp')
- w_mlp_out_grad: float32 [1152, 768], P('dp')
The draws below stay inside these ranges and needn't reach their ends.
Inputs may be any that keep to these rules, and one draw needn't show every extreme that they name: `block_offsets`: each row holds every multiple of 512 below 4096 exactly once.
All inputs are finite; a program needn't handle non-finite values.
Results may differ from the reference program's by a relative error of at most 0.022.
Values may be sent and summed in bfloat16 or wider, within the bound.
No kernel may reach another device: no remote copies, remote signals or barrier semaphores. Data moves between devices by JAX's collectives and lax.ppermute only.
A program may use at most 128 MiB of HBM per device.

```python
import jax
import jax.numpy as jnp
from jax import lax

HEADS = 12
HEAD_DIM = 64
FF = 1152
D = 768
TOK_DEV = 512
LENGTH = 4096
SEQS = 4
N_CTX = 8


def draw_block_offsets(key, part):
    seq_keys = jax.random.split(key, SEQS)
    orders = jax.vmap(lambda one_key: jax.random.permutation(one_key, N_CTX))(seq_keys)
    return (orders * TOK_DEV).astype(jnp.int32)


def levels(key, extent, pieces, low, high):
    loudness = 1.0
    for dim, blocks in pieces:
        heights = jax.random.uniform(jax.random.fold_in(jax.random.fold_in(key, 6), dim), (blocks,), jnp.float32, low / len(pieces), high / len(pieces))
        loudness = loudness * jnp.repeat(jnp.exp(heights), extent[dim] // blocks).reshape((-1,) + (1,) * (len(extent) - 1 - dim))
    return loudness


def centred(key, shape, deviation, most, shards=(), kind=jnp.bfloat16):
    drawn = deviation * jax.random.normal(key, shape, jnp.float32)
    if shards:
        drawn = drawn * levels(key, shape, shards, -0.22, 0.18)
    return jnp.clip(drawn, -most, most).astype(kind)


def setup_inputs(seed: int = 0) -> dict:
    keys = jax.random.split(jax.random.key(seed), 10)
    tokens = centred(keys[0], (SEQS, LENGTH, D), 1.0, 6.0, ((0, 4), (1, 8)))
    cotangent = centred(keys[1], (SEQS, LENGTH, D), 1.0, 6.0, ((0, 4), (1, 8)))
    attn_gain = jnp.clip(1.0 + 0.18 * jax.random.normal(keys[2], (D,), jnp.float32), 0.099609375, 1.8984375).astype(jnp.bfloat16)
    mlp_gain = jnp.clip(1.0 + 0.18 * jax.random.normal(keys[3], (D,), jnp.float32), 0.099609375, 1.8984375).astype(jnp.bfloat16)
    w_qkv = centred(keys[4], (D, 3 * D), D ** -0.5, 0.21875, ((0, 4),))
    w_out = centred(keys[5], (D, D), (max(1, 4 * D // LENGTH)) ** -0.5, 6.0, ((0, 4),))
    w_in = centred(keys[6], (D, 2 * FF), D ** -0.5, 0.21875, ((0, 4),))
    w_mlp_out = centred(keys[7], (FF, D), FF ** -0.5, 0.1875, ((0, 4),))
    block_offsets = draw_block_offsets(jax.random.fold_in(keys[9], 71), 0)
    return dict(tokens=tokens, cotangent=cotangent, attn_gain=attn_gain, mlp_gain=mlp_gain, w_qkv=w_qkv, w_out=w_out, w_in=w_in, w_mlp_out=w_mlp_out, block_offsets=block_offsets)


@jax.custom_vjp
def low(v):
    return lax.optimization_barrier(v.astype(jnp.bfloat16)).astype(jnp.float32)

@jax.custom_vjp
def low_back(v):
    return v

def low_keep(v):
    return (low(v), None)

def low_pass(kept, grad):
    return (grad,)

def back_keep(v):
    return (v, None)

def back_low(kept, grad):
    return (low(grad),)
low.defvjp(low_keep, low_pass)
low_back.defvjp(back_keep, back_low)
rope_base = 160000.0
norm_eps = 1e-05

def highest(left, right):
    return jnp.dot(left, right, precision=lax.Precision.HIGHEST)

def layer_norm(values, gain):
    center = values - lax.optimization_barrier(jnp.mean(values, axis=-1, keepdims=True))
    spread = lax.optimization_barrier(jnp.mean(center * center, axis=-1, keepdims=True))
    return center * lax.rsqrt(spread + norm_eps) * gain

def rotary_tables(positions):
    half_size = HEAD_DIM // 2
    frequency = rope_base ** (-jnp.arange(half_size, dtype=jnp.float32) / half_size)
    angles = positions[:, None] * frequency[None, :]
    cosine = jnp.cos(angles)
    sine_table = jnp.sin(angles)
    return (jnp.concatenate([cosine, cosine], -1), jnp.concatenate([sine_table, sine_table], -1))

def rotate(values, cosine, sine_table):
    half_size = values.shape[-1] // 2
    turned = jnp.concatenate([-values[..., half_size:], values[..., :half_size]], -1)
    return values * cosine[:, None, :] + turned * sine_table[:, None, :]

def forward(inputs, attn_gain, mlp_gain, w_qkv, w_out, w_in, w_mlp_out, cosine, sine_table):
    length = inputs.shape[0]
    scale = HEAD_DIM ** (-0.5)
    normed = low(layer_norm(inputs, attn_gain))
    packed = low_back(highest(normed, w_qkv))
    shaped = packed.reshape(length, 3, HEADS, HEAD_DIM)
    queries = low(rotate(shaped[:, 0], cosine, sine_table))
    keys_all = low(rotate(shaped[:, 1], cosine, sine_table))
    values_all = low(shaped[:, 2])
    block_size = 512 if length % 512 == 0 else length

    def attend(query_block):
        scores = low_back(jnp.einsum('qhd,khd->hqk', query_block, keys_all, precision=lax.Precision.HIGHEST) * scale)
        shifted = jnp.exp(scores - lax.optimization_barrier(jnp.max(scores, axis=-1, keepdims=True)))
        weights = low(shifted / lax.optimization_barrier(jnp.sum(shifted, axis=-1, keepdims=True)))
        return jnp.einsum('hqk,khd->qhd', weights, values_all, precision=lax.Precision.HIGHEST)
    blocks = queries.reshape(length // block_size, block_size, HEADS, HEAD_DIM)
    attended = lax.map(jax.checkpoint(attend), blocks).reshape(length, HEADS * HEAD_DIM)
    attended = low(low_back(attended))
    residual = inputs + low_back(highest(attended, w_out))
    gated_in = low(layer_norm(residual, mlp_gain))
    up_gate = low_back(highest(gated_in, w_in))
    joined = low(jax.nn.gelu(up_gate[:, :FF], approximate=False) * up_gate[:, FF:])
    return residual + low_back(highest(joined, w_mlp_out))

def reference(tokens, cotangent, attn_gain, mlp_gain, w_qkv, w_out, w_in, w_mlp_out, block_offsets):
    params = tuple((item.astype(jnp.float32) for item in (attn_gain, mlp_gain, w_qkv, w_out, w_in, w_mlp_out)))
    local_steps = jnp.arange(TOK_DEV, dtype=jnp.int32)

    def one_sequence(carried, item):
        inputs, upstream, offsets = item
        positions = (offsets.astype(jnp.int32)[:, None] + local_steps[None, :]).reshape(-1).astype(jnp.float32)
        cosine, sine_table = rotary_tables(positions)

        def run(values, gain_one, gain_two, weight_qkv, weight_out, weight_in, weight_down):
            return forward(values, gain_one, gain_two, weight_qkv, weight_out, weight_in, weight_down, cosine, sine_table)
        result, pull = jax.vjp(run, inputs.astype(jnp.float32), *params)
        grads = pull(upstream.astype(jnp.float32))
        updated = tuple((total + grad for total, grad in zip(carried, grads[1:])))
        return (updated, (result.astype(jnp.bfloat16), grads[0]))
    zeros = tuple((jnp.zeros(item.shape, jnp.float32) for item in params))
    totals, (outputs, input_grads) = lax.scan(one_sequence, zeros, (tokens, cotangent, block_offsets))
    return (outputs, input_grads, totals[0], totals[1], totals[2], totals[3], totals[4], totals[5])
```

```python
import functools

import jax
import jax.numpy as jnp
from jax import lax
from jax.experimental import pallas as pl
from jax.experimental.pallas import tpu as pltpu
from jax.sharding import PartitionSpec as P

HEADS = 12
HEAD_DIM = 64
FF = 1152
GROUPS = 4
CHUNKS = HEADS // GROUPS

rope_base = 160000.0
norm_eps = 1e-05


def layer_norm(values, gain):
    center = values - jnp.mean(values, axis=-1, keepdims=True)
    spread = jnp.mean(center * center, axis=-1, keepdims=True)
    return center * lax.rsqrt(spread + norm_eps) * gain


def norm_back(values, gain, upstream):
    _, pull = jax.vjp(layer_norm, values, gain)
    return pull(upstream)


def geglu(packed, hidden_size):
    return jax.nn.gelu(packed[:, :hidden_size], approximate=False) * packed[:, hidden_size:]


def product(left, right, left_dim=1, right_dim=0):
    return lax.dot_general(
        left, right, (((left_dim,), (right_dim,)), ((), ())), preferred_element_type=jnp.float32
    )


def rotate(values, cosine, sine):
    low_half, high_half = values[..., :32, :], values[..., 32:, :]
    return jnp.concatenate(
        [low_half * cosine - high_half * sine, high_half * cosine + low_half * sine], axis=-2
    )


def unrotate(values, cosine, sine):
    low_half, high_half = values[..., :32, :], values[..., 32:, :]
    return jnp.concatenate(
        [low_half * cosine + high_half * sine, high_half * cosine - low_half * sine], axis=-2
    )


def forward_kernel(m, own, *rest):
    others = rest[: m - 1]
    out, low, total, keys = rest[m - 1 :]
    n, _, d, t = own.shape
    parts = [(own, s, 1, 2) for s in range(n)] + [(r, s, 0, 1) for r in others for s in range(n)]
    for i, (ref, s, key_at, _) in enumerate(parts):
        keys[i] = ref[s, key_at].T

    def step(j, _):
        query = own[j, 0]
        top = jnp.full((1, t), -1e30, jnp.float32)
        sums = jnp.zeros((1, t), jnp.float32)
        acc = jnp.zeros((d, t), jnp.float32)
        for i, (ref, s, _, value_at) in enumerate(parts):
            scores = product(keys[i], query)
            new = jnp.maximum(top, jnp.max(scores, axis=0, keepdims=True))
            weights = jnp.exp(scores - new)
            rescale = jnp.exp(top - new)
            sums = sums * rescale + jnp.sum(weights, axis=0, keepdims=True)
            acc = acc * rescale + product(ref[s, value_at], weights.astype(jnp.bfloat16))
            top = new
        done = acc / sums
        out[j] = done
        low[j] = done.astype(jnp.bfloat16)
        total[j] = top + jnp.log(sums)
        return 0

    lax.fori_loop(0, n, step, 0)


def attend(own, others):
    n, _, d, t = own.shape
    m = 1 + len(others)
    pairs = n * t * m * n * t
    return pl.pallas_call(
        functools.partial(forward_kernel, m),
        out_shape=(
            jax.ShapeDtypeStruct((n, d, t), jnp.float32),
            jax.ShapeDtypeStruct((n, d, t), jnp.bfloat16),
            jax.ShapeDtypeStruct((n, 1, t), jnp.float32),
        ),
        scratch_shapes=[pltpu.VMEM((m * n, t, d), jnp.bfloat16)],
        cost_estimate=pl.CostEstimate(
            flops=4 * 4 * d * pairs, transcendentals=pairs, bytes_accessed=2 * 10**6
        ),
        name="attend",
    )(own, *others)


def backward_kernel(m, own, *rest):
    others = rest[: m - 1]
    upstream, out, total, query_grad, *more = rest[m - 1 :]
    grads = more[:m]
    acc, query_rows, upstream_rows, delta = more[m:]
    n, _, d, t = own.shape
    for s in range(n):
        query_rows[s] = own[s, 0].T
        upstream_rows[s] = upstream[s].T
        delta[s] = jnp.sum(upstream[s].astype(jnp.float32) * out[s], axis=0, keepdims=True)
        acc[s] = jnp.zeros((d, t), jnp.float32)
    places = [(1, 2)] + [(0, 1)] * (m - 1)
    for ref, (key_at, value_at), grad in zip((own,) + tuple(others), places, grads):

        def step(s, _):
            keys = ref[s, key_at]
            key_rows = keys.T
            value_rows = ref[s, value_at].T
            key_grad = jnp.zeros((t, d), jnp.float32)
            value_grad = jnp.zeros((t, d), jnp.float32)
            for j in range(n):
                probs = jnp.exp(product(key_rows, own[j, 0]) - total[j])
                prob_grad = product(value_rows, upstream[j])
                score_grad = (probs * (prob_grad - delta[j])).astype(jnp.bfloat16)
                value_grad = value_grad + product(probs.astype(jnp.bfloat16), upstream_rows[j])
                key_grad = key_grad + product(score_grad, query_rows[j])
                acc[j] += product(keys, score_grad)
            grad[s, 0] = key_grad.T.astype(jnp.bfloat16)
            grad[s, 1] = value_grad.T.astype(jnp.bfloat16)
            return 0

        lax.fori_loop(0, n, step, 0)
    for s in range(n):
        query_grad[s] = (acc[s] * d**-0.5).astype(jnp.bfloat16)


def attend_back(own, others, upstream, out, total):
    n, _, d, t = own.shape
    m = 1 + len(others)
    pairs = n * t * m * n * t
    return pl.pallas_call(
        functools.partial(backward_kernel, m),
        out_shape=(jax.ShapeDtypeStruct((n, d, t), jnp.bfloat16),)
        + tuple(jax.ShapeDtypeStruct((n, 2, d, t), jnp.bfloat16) for _ in range(m)),
        scratch_shapes=[
            pltpu.VMEM((n, d, t), jnp.float32),
            pltpu.VMEM((n, t, d), jnp.bfloat16),
            pltpu.VMEM((n, t, d), jnp.bfloat16),
            pltpu.VMEM((n, 1, t), jnp.float32),
        ],
        cost_estimate=pl.CostEstimate(
            flops=10 * 4 * d * pairs, transcendentals=pairs, bytes_accessed=4 * 10**6
        ),
        name="attend_back",
    )(own, *others, upstream, out, total)


def exchange(values):
    count = lax.axis_size("ctx") // GROUPS
    groups = [[g * count + y for g in range(GROUPS)] for y in range(count)]
    return lax.all_to_all(values, "ctx", 0, 0, axis_index_groups=groups)


def across(values, by):
    count = lax.axis_size("ctx") // GROUPS
    pairs = [
        (g * count + y, g * count + (y + by) % count) for g in range(GROUPS) for y in range(count)
    ]
    return lax.ppermute(values, "ctx", pairs)


def gathered(value):
    return lax.all_gather(value, "dp", axis=0, tiled=True)


def reduced(value):
    part = lax.psum_scatter(value.astype(jnp.bfloat16), "dp", scatter_dimension=0, tiled=True)
    return lax.psum(part, "ctx").astype(jnp.float32)


def body(tokens, cotangent, attn_gain, mlp_gain, w_qkv, w_out, w_in, w_mlp_out, block_offsets):
    width = HEADS * HEAD_DIM
    part = GROUPS * HEAD_DIM
    inputs = tokens[0].astype(jnp.float32)
    t = inputs.shape[0]
    m = lax.axis_size("ctx") // GROUPS
    positions = (block_offsets[0, 0] + jnp.arange(t, dtype=jnp.int32)).astype(jnp.float32)
    half = HEAD_DIM // 2
    frequency = rope_base ** (-jnp.arange(half, dtype=jnp.float32) / half)
    angles = frequency[:, None] * positions[None, :]
    cosine, sine = jnp.cos(angles), jnp.sin(angles)

    gains = lax.all_gather(jnp.stack([attn_gain, mlp_gain]), "dp", axis=1, tiled=True)
    local_qkv = w_qkv.reshape(-1, 3, CHUNKS, part)
    weights_qkv = [gathered(local_qkv[:, :, i].reshape(-1, 3 * part)) for i in range(CHUNKS)]
    weight_out, weight_in, weight_down = gathered(w_out), gathered(w_in), gathered(w_mlp_out)
    first_gain = gains[0].astype(jnp.float32)
    second_gain = gains[1].astype(jnp.float32)

    normed = layer_norm(inputs, first_gain).astype(jnp.bfloat16)
    kept, lows = [], []
    for i in range(CHUNKS):
        packed = product(weights_qkv[i], normed, 0, 1).reshape(3, GROUPS, HEAD_DIM, t)
        queries = rotate(packed[0], cosine, sine).astype(jnp.bfloat16) * HEAD_DIM**-0.5
        keys = rotate(packed[1], cosine, sine).astype(jnp.bfloat16)
        values = packed[2].astype(jnp.bfloat16)
        own = exchange(jnp.stack([queries, keys, values], axis=1))
        others = [across(own[:, 1:], by) for by in range(1, m)]
        out, low, total = attend(own, others)
        lows.append(exchange(low).reshape(part, t))
        kept.append((own, others, out, total))
    attended = jnp.concatenate(lows, axis=0)

    residual = inputs + product(attended, weight_out, 0, 0)
    mlp_normed = layer_norm(residual, second_gain).astype(jnp.bfloat16)
    up_gate = product(mlp_normed, weight_in)
    joined = geglu(up_gate, FF).astype(jnp.bfloat16)
    mixed = (residual + product(joined, weight_down)).astype(jnp.bfloat16)[None]

    upstream_low = cotangent[0]
    upstream = upstream_low.astype(jnp.float32)
    grad_joined = product(upstream_low, weight_down, 1, 1)
    _, glu_pull = jax.vjp(lambda packed_in: geglu(packed_in, FF), up_gate)
    grad_up_gate = glu_pull(grad_joined)[0].astype(jnp.bfloat16)
    grad_mlp_normed = product(grad_up_gate, weight_in, 1, 1)
    grad_residual_norm, grad_gain_two = norm_back(residual, second_gain, grad_mlp_normed)
    grad_residual = upstream + grad_residual_norm
    residual_low = grad_residual.astype(jnp.bfloat16)
    grad_attended = (
        product(weight_out, residual_low, 1, 1)
        .astype(jnp.bfloat16)
        .reshape(CHUNKS, GROUPS, HEAD_DIM, t)
    )
    total_down = reduced(product(joined, upstream_low, 0, 0))
    total_in = reduced(product(mlp_normed, grad_up_gate, 0, 0))
    total_out = reduced(product(attended, residual_low, 1, 0))

    grad_normed = 0.0
    totals_qkv = []
    for i in range(CHUNKS):
        own, others, out, total = kept[i]
        query_grad, own_grad, *other_grads = attend_back(
            own, others, exchange(grad_attended[i]), out, total
        )
        sums = own_grad.astype(jnp.float32)
        for by, grad in zip(range(1, m), other_grads):
            sums = sums + across(grad, -by).astype(jnp.float32)
        back = exchange(
            jnp.concatenate([query_grad[:, None], sums.astype(jnp.bfloat16)], axis=1)
        ).astype(jnp.float32)
        grad_packed = (
            jnp.stack(
                [
                    unrotate(back[:, 0], cosine, sine),
                    unrotate(back[:, 1], cosine, sine),
                    back[:, 2],
                ]
            )
            .astype(jnp.bfloat16)
            .reshape(3 * part, t)
        )
        totals_qkv.append(reduced(product(normed, grad_packed, 0, 1)).reshape(-1, 3, 1, part))
        grad_normed = grad_normed + product(grad_packed, weights_qkv[i], 0, 1)
    total_qkv = jnp.concatenate(totals_qkv, axis=2).reshape(-1, 3 * width)
    grad_inputs_norm, grad_gain_one = norm_back(inputs, first_gain, grad_normed)
    tokens_grad = (grad_residual + grad_inputs_norm)[None]

    gain_rows = attn_gain.shape[0]
    gain_sums = lax.psum(jnp.stack([grad_gain_one, grad_gain_two]), ("ctx", "dp"))
    gain_sums = lax.dynamic_slice_in_dim(gain_sums, lax.axis_index("dp") * gain_rows, gain_rows, 1)
    return (
        mixed,
        tokens_grad,
        gain_sums[0],
        gain_sums[1],
        total_qkv,
        total_out,
        total_in,
        total_down,
    )


def solution(mesh):
    return jax.shard_map(
        body,
        mesh=mesh,
        in_specs=(
            P("dp", "ctx", None),
            P("dp", "ctx", None),
            P("dp"),
            P("dp"),
            P("dp", None),
            P("dp", None),
            P("dp", None),
            P("dp", None),
            P("dp", "ctx"),
        ),
        out_specs=(
            P("dp", "ctx", None),
            P("dp", "ctx", None),
            P("dp"),
            P("dp"),
            P("dp", None),
            P("dp", None),
            P("dp", None),
            P("dp", None),
        ),
        check_vma=False,
    )
```

```python
import functools

import jax
import jax.numpy as jnp
from jax import lax
from jax.experimental import pallas as pl
from jax.experimental.pallas import tpu as pltpu
from jax.sharding import PartitionSpec as P


HEADS = 12
HEAD_DIM = 64
FF = 1152
GROUPS = 4
CHUNKS = HEADS // GROUPS

rope_base = 160000.0
norm_eps = 1e-05


def layer_norm(values, gain):
    center = values - jnp.mean(values, axis=-1, keepdims=True)
    spread = jnp.mean(center * center, axis=-1, keepdims=True)
    return center * lax.rsqrt(spread + norm_eps) * gain


def norm_back(values, gain, upstream):
    _, pull = jax.vjp(layer_norm, values, gain)
    return pull(upstream)


def geglu(packed, hidden_size):
    return jax.nn.gelu(packed[:, :hidden_size], approximate=False) * packed[:, hidden_size:]


def product(left, right, left_dim=1, right_dim=0):
    return lax.dot_general(
        left, right, (((left_dim,), (right_dim,)), ((), ())), preferred_element_type=jnp.float32
    )


def rotate(values, cosine, sine):
    low_half, high_half = values[..., :32, :], values[..., 32:, :]
    return jnp.concatenate(
        [low_half * cosine - high_half * sine, high_half * cosine + low_half * sine], axis=-2
    )


def unrotate(values, cosine, sine):
    low_half, high_half = values[..., :32, :], values[..., 32:, :]
    return jnp.concatenate(
        [low_half * cosine + high_half * sine, high_half * cosine - low_half * sine], axis=-2
    )


def forward_kernel(m, own, *rest):
    others = rest[: m - 1]
    out, low, total, keys = rest[m - 1 :]
    n, _, d, t = own.shape
    parts = [(own, s, 1, 2) for s in range(n)] + [(r, s, 0, 1) for r in others for s in range(n)]
    for i, (ref, s, key_at, _) in enumerate(parts):
        keys[i] = ref[s, key_at].T

    def step(j, _):
        query = own[j, 0]
        top = jnp.full((1, t), -1e30, jnp.float32)
        sums = jnp.zeros((1, t), jnp.float32)
        acc = jnp.zeros((d, t), jnp.float32)
        for i, (ref, s, _, value_at) in enumerate(parts):
            scores = product(keys[i], query)
            new = jnp.maximum(top, jnp.max(scores, axis=0, keepdims=True))
            weights = jnp.exp(scores - new)
            rescale = jnp.exp(top - new)
            sums = sums * rescale + jnp.sum(weights, axis=0, keepdims=True)
            acc = acc * rescale + product(ref[s, value_at], weights.astype(jnp.bfloat16))
            top = new
        done = acc / sums
        out[j] = done
        low[j] = done.astype(jnp.bfloat16)
        total[j] = top + jnp.log(sums)
        return 0

    lax.fori_loop(0, n, step, 0)


def attend(own, others):
    n, _, d, t = own.shape
    m = 1 + len(others)
    pairs = n * t * m * n * t
    return pl.pallas_call(
        functools.partial(forward_kernel, m),
        out_shape=(
            jax.ShapeDtypeStruct((n, d, t), jnp.float32),
            jax.ShapeDtypeStruct((n, d, t), jnp.bfloat16),
            jax.ShapeDtypeStruct((n, 1, t), jnp.float32),
        ),
        scratch_shapes=[pltpu.VMEM((m * n, t, d), jnp.bfloat16)],
        cost_estimate=pl.CostEstimate(
            flops=4 * 4 * d * pairs, transcendentals=pairs, bytes_accessed=2 * 10**6
        ),
        name="attend",
    )(own, *others)


def backward_kernel(m, own, *rest):
    others = rest[: m - 1]
    upstream, out, total, query_grad, *more = rest[m - 1 :]
    grads = more[:m]
    acc, query_rows, upstream_rows, delta = more[m:]
    n, _, d, t = own.shape
    for s in range(n):
        query_rows[s] = own[s, 0].T
        upstream_rows[s] = upstream[s].T
        delta[s] = jnp.sum(upstream[s].astype(jnp.float32) * out[s], axis=0, keepdims=True)
        acc[s] = jnp.zeros((d, t), jnp.float32)
    places = [(1, 2)] + [(0, 1)] * (m - 1)
    for ref, (key_at, value_at), grad in zip((own,) + tuple(others), places, grads):

        def step(s, _):
            keys = ref[s, key_at]
            key_rows = keys.T
            value_rows = ref[s, value_at].T
            key_grad = jnp.zeros((t, d), jnp.float32)
            value_grad = jnp.zeros((t, d), jnp.float32)
            for j in range(n):
                probs = jnp.exp(product(key_rows, own[j, 0]) - total[j])
                prob_grad = product(value_rows, upstream[j])
                score_grad = (probs * (prob_grad - delta[j])).astype(jnp.bfloat16)
                value_grad = value_grad + product(probs.astype(jnp.bfloat16), upstream_rows[j])
                key_grad = key_grad + product(score_grad, query_rows[j])
                acc[j] += product(keys, score_grad)
            grad[s, 0] = key_grad.T.astype(jnp.bfloat16)
            grad[s, 1] = value_grad.T.astype(jnp.bfloat16)
            return 0

        lax.fori_loop(0, n, step, 0)
    for s in range(n):
        query_grad[s] = acc[s] * d**-0.5


def attend_back(own, others, upstream, out, total):
    n, _, d, t = own.shape
    m = 1 + len(others)
    pairs = n * t * m * n * t
    return pl.pallas_call(
        functools.partial(backward_kernel, m),
        out_shape=(jax.ShapeDtypeStruct((n, d, t), jnp.float32),)
        + tuple(jax.ShapeDtypeStruct((n, 2, d, t), jnp.bfloat16) for _ in range(m)),
        scratch_shapes=[
            pltpu.VMEM((n, d, t), jnp.float32),
            pltpu.VMEM((n, t, d), jnp.bfloat16),
            pltpu.VMEM((n, t, d), jnp.bfloat16),
            pltpu.VMEM((n, 1, t), jnp.float32),
        ],
        cost_estimate=pl.CostEstimate(
            flops=10 * 4 * d * pairs, transcendentals=pairs, bytes_accessed=4 * 10**6
        ),
        name="attend_back",
    )(own, *others, upstream, out, total)


def exchange(values):
    return lax.all_to_all(values, "ctx", 0, 0, axis_index_groups=alike())


def alike():
    count = lax.axis_size("ctx") // GROUPS
    return [[g * count + y for g in range(GROUPS)] for y in range(count)]


def across(values, by):
    count = lax.axis_size("ctx") // GROUPS
    pairs = [
        (g * count + y, g * count + (y + by) % count) for g in range(GROUPS) for y in range(count)
    ]
    return lax.ppermute(values, "ctx", pairs)


def gathered(value):
    return lax.all_gather(value, "dp", axis=0, tiled=True)


def reduced(value):
    part = lax.psum_scatter(value.astype(jnp.bfloat16), "dp", scatter_dimension=0, tiled=True)
    return lax.psum(part, "ctx").astype(jnp.float32)


def swapped(values, axis, bit):
    count = lax.axis_size(axis)
    return lax.ppermute(values, axis, [(i, i ^ bit) for i in range(count)])


def by_group(value):
    count = lax.axis_size("ctx") // GROUPS
    group = lax.axis_index("ctx") // count
    value = value[None]
    bit = 1
    while bit < GROUPS:
        other = swapped(value, "ctx", bit * count)
        value = jnp.where(
            (group // bit) % 2 == 0,
            jnp.concatenate([value, other]),
            jnp.concatenate([other, value]),
        )
        bit *= 2
    return value


def reduced_heads(value):
    size = lax.axis_size("dp")
    place = lax.axis_index("dp")
    value = value.reshape(size, value.shape[0] // size, value.shape[1])
    bit = 1
    while bit < size:
        value = value.reshape(value.shape[0] // 2, 2, *value.shape[1:])
        mine = (place // bit) % 2
        keep = lax.dynamic_index_in_dim(value, mine, 1, keepdims=False)
        send = lax.dynamic_index_in_dim(value, 1 - mine, 1, keepdims=False)
        value = keep + swapped(send.astype(jnp.bfloat16), "dp", bit).astype(jnp.float32)
        bit *= 2
    value = value[0]
    count = lax.axis_size("ctx") // GROUPS
    bit = 1
    while bit < count:
        value = value.astype(jnp.bfloat16)
        value = value.astype(jnp.float32) + swapped(value, "ctx", bit).astype(jnp.float32)
        bit *= 2
    return by_group(value.astype(jnp.bfloat16)).astype(jnp.float32)


def tables(positions):
    half = HEAD_DIM // 2
    frequency = rope_base ** (-jnp.arange(half, dtype=jnp.float32) / half)
    angles = frequency[:, None] * positions[..., None, :]
    return jnp.cos(angles), jnp.sin(angles)


def layer(tokens, cotangent, attn_gain, mlp_gain, w_qkv, w_out, w_in, w_mlp_out, block_offsets):
    width = HEADS * HEAD_DIM
    part = GROUPS * HEAD_DIM
    inputs = tokens[0].astype(jnp.float32)
    t = inputs.shape[0]
    m = lax.axis_size("ctx") // GROUPS
    steps = jnp.arange(t, dtype=jnp.int32)
    cosine, sine = tables((block_offsets[0, 0] + steps).astype(jnp.float32))

    gains = lax.all_gather(jnp.stack([attn_gain, mlp_gain]), "dp", axis=1, tiled=True)
    local_qkv = w_qkv.reshape(-1, 3, CHUNKS, part)
    weights_qkv = [gathered(local_qkv[:, :, i].reshape(-1, 3 * part)) for i in range(CHUNKS)]
    weight_out, weight_in, weight_down = gathered(w_out), gathered(w_in), gathered(w_mlp_out)
    first_gain = gains[0].astype(jnp.float32)
    second_gain = gains[1].astype(jnp.float32)

    normed = layer_norm(inputs, first_gain).astype(jnp.bfloat16)
    kept, lows = [], []
    for i in range(CHUNKS):
        packed = product(weights_qkv[i], normed, 0, 1).reshape(3, GROUPS, HEAD_DIM, t)
        queries = rotate(packed[0], cosine, sine).astype(jnp.bfloat16) * HEAD_DIM**-0.5
        keys = rotate(packed[1], cosine, sine).astype(jnp.bfloat16)
        values = packed[2].astype(jnp.bfloat16)
        own = exchange(jnp.stack([queries, keys, values], axis=1))
        others = [across(own[:, 1:], by) for by in range(1, m)]
        out, low, total = attend(own, others)
        lows.append(exchange(low).reshape(part, t))
        kept.append((own, others, out, total))
    attended = jnp.concatenate(lows, axis=0)
    normed_here = lax.all_gather(normed, "ctx", axis=0, axis_index_groups=alike())
    offsets = by_group(block_offsets[0])[:, 0]
    cosine_here, sine_here = tables((offsets[:, None] + steps).astype(jnp.float32))

    residual = inputs + product(attended, weight_out, 0, 0)
    mlp_normed = layer_norm(residual, second_gain).astype(jnp.bfloat16)
    up_gate = product(mlp_normed, weight_in)
    joined = geglu(up_gate, FF).astype(jnp.bfloat16)
    mixed = (residual + product(joined, weight_down)).astype(jnp.bfloat16)[None]

    upstream_low = cotangent[0]
    upstream = upstream_low.astype(jnp.float32)
    grad_joined = product(upstream_low, weight_down, 1, 1)
    _, glu_pull = jax.vjp(lambda packed_in: geglu(packed_in, FF), up_gate)
    grad_up_gate = glu_pull(grad_joined)[0].astype(jnp.bfloat16)
    grad_mlp_normed = product(grad_up_gate, weight_in, 1, 1)
    grad_residual_norm, grad_gain_two = norm_back(residual, second_gain, grad_mlp_normed)
    grad_residual = upstream + grad_residual_norm
    residual_low = grad_residual.astype(jnp.bfloat16)
    grad_attended = (
        product(weight_out, residual_low, 1, 1)
        .astype(jnp.bfloat16)
        .reshape(CHUNKS, GROUPS, HEAD_DIM, t)
    )
    total_down = reduced(product(joined, upstream_low, 0, 0))
    total_in = reduced(product(mlp_normed, grad_up_gate, 0, 0))
    total_out = reduced(product(attended, residual_low, 1, 0))

    ups = []
    for i in range(CHUNKS):
        ups.append(exchange(grad_attended[i]))
    grad_normed = 0.0
    totals_qkv, packs, grads = [], [], []
    for i in range(CHUNKS):
        own, others, out, total = kept[i]
        if i > 1:
            ups[i], packs[i - 2], grads[i - 2] = lax.optimization_barrier(
                (ups[i], packs[i - 2], grads[i - 2])
            )
        query_grad, own_grad, *other_grads = attend_back(own, others, ups[i], out, total)
        sums = own_grad.astype(jnp.float32)
        moved = [across(grad, -by) for by, grad in zip(range(1, m), other_grads)]
        for grad in moved:
            sums = sums + grad.astype(jnp.float32)
        grad_packed = jnp.stack(
            [
                unrotate(query_grad, cosine_here, sine_here),
                unrotate(sums[:, 0], cosine_here, sine_here),
                sums[:, 1],
            ],
            axis=1,
        ).astype(jnp.bfloat16)
        packs.append(grad_packed)
        heads_grad = lax.dot_general(
            normed_here,
            grad_packed.reshape(GROUPS, 3 * HEAD_DIM, t),
            (((0, 1), (0, 2)), ((), ())),
            preferred_element_type=jnp.float32,
        )
        grads.append(heads_grad)
    for i in range(CHUNKS):
        back = exchange(packs[i])
        totals_qkv.append(reduced_heads(grads[i]))
        back = back.transpose(1, 0, 2, 3).reshape(3 * part, t)
        grad_normed = grad_normed + product(back, weights_qkv[i], 0, 1)
    total_qkv = jnp.stack(totals_qkv).reshape(CHUNKS, GROUPS, -1, 3, HEAD_DIM)
    total_qkv = total_qkv.transpose(2, 3, 0, 1, 4).reshape(-1, 3 * width)
    grad_inputs_norm, grad_gain_one = norm_back(inputs, first_gain, grad_normed)
    tokens_grad = (grad_residual + grad_inputs_norm)[None]

    gain_rows = attn_gain.shape[0]
    gain_parts = lax.all_gather(jnp.stack([grad_gain_one, grad_gain_two]), ("ctx", "dp"))
    gain_parts = lax.dynamic_slice_in_dim(
        gain_parts, lax.axis_index("dp") * gain_rows, gain_rows, 2
    )
    gain_sums = jnp.sum(gain_parts, axis=0)
    return (
        mixed,
        tokens_grad,
        gain_sums[0],
        gain_sums[1],
        total_qkv,
        total_out,
        total_in,
        total_down,
    )


def solution(mesh):
    return jax.shard_map(
        layer,
        mesh=mesh,
        in_specs=(
            P("dp", "ctx", None),
            P("dp", "ctx", None),
            P("dp"),
            P("dp"),
            P("dp", None),
            P("dp", None),
            P("dp", None),
            P("dp", None),
            P("dp", "ctx"),
        ),
        out_specs=(
            P("dp", "ctx", None),
            P("dp", "ctx", None),
            P("dp"),
            P("dp"),
            P("dp", None),
            P("dp", None),
            P("dp", None),
            P("dp", None),
        ),
        check_vma=False,
    )
```

```python
import functools

import jax
import jax.numpy as jnp
from jax import lax
from jax.experimental import pallas as pl
from jax.experimental.pallas import tpu as pltpu
from jax.sharding import PartitionSpec as P


HEADS = 12
HEAD_DIM = 64
FF = 1152
GROUPS = 4
CHUNKS = HEADS // GROUPS

rope_base = 160000.0
norm_eps = 1e-05


def layer_norm(values, gain):
    center = values - jnp.mean(values, axis=-1, keepdims=True)
    spread = jnp.mean(center * center, axis=-1, keepdims=True)
    return center * lax.rsqrt(spread + norm_eps) * gain


def norm_back(values, gain, upstream):
    _, pull = jax.vjp(layer_norm, values, gain)
    return pull(upstream)


def geglu(packed, hidden_size):
    return jax.nn.gelu(packed[:, :hidden_size], approximate=False) * packed[:, hidden_size:]


def product(left, right, left_dim=1, right_dim=0):
    return lax.dot_general(
        left, right, (((left_dim,), (right_dim,)), ((), ())), preferred_element_type=jnp.float32
    )


def rotate(values, cosine, sine):
    low_half, high_half = values[..., :32, :], values[..., 32:, :]
    return jnp.concatenate(
        [low_half * cosine - high_half * sine, high_half * cosine + low_half * sine], axis=-2
    )


def unrotate(values, cosine, sine):
    low_half, high_half = values[..., :32, :], values[..., 32:, :]
    return jnp.concatenate(
        [low_half * cosine + high_half * sine, high_half * cosine - low_half * sine], axis=-2
    )


def forward_kernel(m, own, *rest):
    others = rest[: m - 1]
    out, low, total, keys = rest[m - 1 :]
    n, _, d, t = own.shape
    parts = [(own, s, 1, 2) for s in range(n)] + [(r, s, 0, 1) for r in others for s in range(n)]
    for i, (ref, s, key_at, _) in enumerate(parts):
        keys[i] = ref[s, key_at].T

    def step(j, _):
        query = own[j, 0]
        top = jnp.full((1, t), -1e30, jnp.float32)
        sums = jnp.zeros((1, t), jnp.float32)
        acc = jnp.zeros((d, t), jnp.float32)
        for i, (ref, s, _, value_at) in enumerate(parts):
            scores = product(keys[i], query)
            new = jnp.maximum(top, jnp.max(scores, axis=0, keepdims=True))
            weights = jnp.exp(scores - new)
            rescale = jnp.exp(top - new)
            sums = sums * rescale + jnp.sum(weights, axis=0, keepdims=True)
            acc = acc * rescale + product(ref[s, value_at], weights.astype(jnp.bfloat16))
            top = new
        done = acc / sums
        out[j] = done
        low[j] = done.astype(jnp.bfloat16)
        total[j] = top + jnp.log(sums)
        return 0

    lax.fori_loop(0, n, step, 0)


def attend(own, others):
    n, _, d, t = own.shape
    m = 1 + len(others)
    pairs = n * t * m * n * t
    return pl.pallas_call(
        functools.partial(forward_kernel, m),
        out_shape=(
            jax.ShapeDtypeStruct((n, d, t), jnp.float32),
            jax.ShapeDtypeStruct((n, d, t), jnp.bfloat16),
            jax.ShapeDtypeStruct((n, 1, t), jnp.float32),
        ),
        scratch_shapes=[pltpu.VMEM((m * n, t, d), jnp.bfloat16)],
        cost_estimate=pl.CostEstimate(
            flops=4 * 4 * d * pairs, transcendentals=pairs, bytes_accessed=2 * 10**6
        ),
        name="attend",
    )(own, *others)


def backward_kernel(m, own, *rest):
    others = rest[: m - 1]
    upstream, out, total, query_grad, *more = rest[m - 1 :]
    grads = more[:m]
    acc, query_rows, upstream_rows, delta = more[m:]
    n, _, d, t = own.shape
    for s in range(n):
        query_rows[s] = own[s, 0].T
        upstream_rows[s] = upstream[s].T
        delta[s] = jnp.sum(upstream[s].astype(jnp.float32) * out[s], axis=0, keepdims=True)
        acc[s] = jnp.zeros((d, t), jnp.float32)
    places = [(1, 2)] + [(0, 1)] * (m - 1)
    for ref, (key_at, value_at), grad in zip((own,) + tuple(others), places, grads):

        def step(s, _):
            keys = ref[s, key_at]
            key_rows = keys.T
            value_rows = ref[s, value_at].T
            key_grad = jnp.zeros((t, d), jnp.float32)
            value_grad = jnp.zeros((t, d), jnp.float32)
            for j in range(n):
                probs = jnp.exp(product(key_rows, own[j, 0]) - total[j])
                prob_grad = product(value_rows, upstream[j])
                score_grad = (probs * (prob_grad - delta[j])).astype(jnp.bfloat16)
                value_grad = value_grad + product(probs.astype(jnp.bfloat16), upstream_rows[j])
                key_grad = key_grad + product(score_grad, query_rows[j])
                acc[j] += product(keys, score_grad)
            grad[s, 0] = key_grad.T.astype(jnp.bfloat16)
            grad[s, 1] = value_grad.T.astype(jnp.bfloat16)
            return 0

        lax.fori_loop(0, n, step, 0)
    for s in range(n):
        query_grad[s] = acc[s] * d**-0.5


def attend_back(own, others, upstream, out, total):
    n, _, d, t = own.shape
    m = 1 + len(others)
    pairs = n * t * m * n * t
    return pl.pallas_call(
        functools.partial(backward_kernel, m),
        out_shape=(jax.ShapeDtypeStruct((n, d, t), jnp.float32),)
        + tuple(jax.ShapeDtypeStruct((n, 2, d, t), jnp.bfloat16) for _ in range(m)),
        scratch_shapes=[
            pltpu.VMEM((n, d, t), jnp.float32),
            pltpu.VMEM((n, t, d), jnp.bfloat16),
            pltpu.VMEM((n, t, d), jnp.bfloat16),
            pltpu.VMEM((n, 1, t), jnp.float32),
        ],
        cost_estimate=pl.CostEstimate(
            flops=10 * 4 * d * pairs, transcendentals=pairs, bytes_accessed=4 * 10**6
        ),
        name="attend_back",
    )(own, *others, upstream, out, total)


def exchange(values):
    return lax.all_to_all(values, "ctx", 0, 0, axis_index_groups=alike())


def alike():
    count = lax.axis_size("ctx") // GROUPS
    return [[g * count + y for g in range(GROUPS)] for y in range(count)]


def across(values, by):
    count = lax.axis_size("ctx") // GROUPS
    pairs = [
        (g * count + y, g * count + (y + by) % count) for g in range(GROUPS) for y in range(count)
    ]
    return lax.ppermute(values, "ctx", pairs)


def gathered(value):
    return lax.all_gather(value, "dp", axis=0, tiled=True)


def reduced(value):
    part = lax.psum_scatter(value.astype(jnp.bfloat16), "dp", scatter_dimension=0, tiled=True)
    return lax.psum(part, "ctx").astype(jnp.float32)


def swapped(values, axis, bit):
    count = lax.axis_size(axis)
    return lax.ppermute(values, axis, [(i, i ^ bit) for i in range(count)])


def by_group(value):
    count = lax.axis_size("ctx") // GROUPS
    group = lax.axis_index("ctx") // count
    value = value[None]
    bit = 1
    while bit < GROUPS:
        other = swapped(value, "ctx", bit * count)
        value = jnp.where(
            (group // bit) % 2 == 0,
            jnp.concatenate([value, other]),
            jnp.concatenate([other, value]),
        )
        bit *= 2
    return value


def reduced_heads(value):
    size = lax.axis_size("dp")
    place = lax.axis_index("dp")
    value = value.reshape(size, value.shape[0] // size, value.shape[1])
    bit = 1
    while bit < size:
        value = value.reshape(value.shape[0] // 2, 2, *value.shape[1:])
        mine = (place // bit) % 2
        keep = lax.dynamic_index_in_dim(value, mine, 1, keepdims=False)
        send = lax.dynamic_index_in_dim(value, 1 - mine, 1, keepdims=False)
        value = keep + swapped(send.astype(jnp.bfloat16), "dp", bit).astype(jnp.float32)
        bit *= 2
    value = value[0]
    count = lax.axis_size("ctx") // GROUPS
    bit = 1
    while bit < count:
        value = value.astype(jnp.bfloat16)
        value = value.astype(jnp.float32) + swapped(value, "ctx", bit).astype(jnp.float32)
        bit *= 2
    return by_group(value.astype(jnp.bfloat16)).astype(jnp.float32)


def tables(positions):
    half = HEAD_DIM // 2
    frequency = rope_base ** (-jnp.arange(half, dtype=jnp.float32) / half)
    angles = frequency[:, None] * positions[..., None, :]
    return jnp.cos(angles), jnp.sin(angles)


def layer(tokens, cotangent, attn_gain, mlp_gain, w_qkv, w_out, w_in, w_mlp_out, block_offsets):
    width = HEADS * HEAD_DIM
    part = GROUPS * HEAD_DIM
    inputs = tokens[0].astype(jnp.float32)
    t = inputs.shape[0]
    m = lax.axis_size("ctx") // GROUPS
    steps = jnp.arange(t, dtype=jnp.int32)
    cosine, sine = tables((block_offsets[0, 0] + steps).astype(jnp.float32))

    gains = lax.all_gather(jnp.stack([attn_gain, mlp_gain]), "dp", axis=1, tiled=True)
    local_qkv = w_qkv.reshape(-1, 3, CHUNKS, part)
    weights_qkv = []
    for i in range(CHUNKS):
        weights_qkv.append(gathered(local_qkv[:, :, i].reshape(-1, 3 * part)))
    weight_out = gathered(w_out)
    weight_in = gathered(w_in)
    weight_down = gathered(w_mlp_out)
    offsets = by_group(block_offsets[0])
    first_gain = gains[0].astype(jnp.float32)
    second_gain = gains[1].astype(jnp.float32)

    normed = layer_norm(inputs, first_gain).astype(jnp.bfloat16)
    normed_next = normed
    kept, lows = [], []
    for i in range(CHUNKS):
        packed = product(weights_qkv[i], normed_next, 0, 1).reshape(3, GROUPS, HEAD_DIM, t)
        queries = rotate(packed[0], cosine, sine).astype(jnp.bfloat16) * HEAD_DIM**-0.5
        keys = rotate(packed[1], cosine, sine).astype(jnp.bfloat16)
        values = packed[2].astype(jnp.bfloat16)
        sent, normed_next = lax.optimization_barrier(
            (jnp.stack([queries, keys, values], axis=1), normed_next)
        )
        own = exchange(sent)
        if i == 0:
            own, offsets = lax.optimization_barrier((own, offsets))
        others = [across(own[:, 1:], by) for by in range(1, m)]
        out, low, total = attend(own, others)
        lows.append(exchange(low).reshape(part, t))
        kept.append((own, others, out, total))
    attended = jnp.concatenate(lows, axis=0)
    normed_here = lax.all_gather(normed, "ctx", axis=0, axis_index_groups=alike())
    cosine_here, sine_here = tables((offsets + steps).astype(jnp.float32))

    residual = inputs + product(attended, weight_out, 0, 0)
    mlp_normed = layer_norm(residual, second_gain).astype(jnp.bfloat16)
    up_gate = product(mlp_normed, weight_in)
    joined = geglu(up_gate, FF).astype(jnp.bfloat16)
    mixed = (residual + product(joined, weight_down)).astype(jnp.bfloat16)[None]

    upstream_low = cotangent[0]
    upstream = upstream_low.astype(jnp.float32)
    grad_down = product(joined, upstream_low, 0, 0).astype(jnp.bfloat16)
    upstream_low, grad_down = lax.optimization_barrier((upstream_low, grad_down))
    total_down = reduced(grad_down)
    grad_joined = product(upstream_low, weight_down, 1, 1)
    _, glu_pull = jax.vjp(lambda packed_in: geglu(packed_in, FF), up_gate)
    grad_up_gate = glu_pull(grad_joined)[0].astype(jnp.bfloat16)
    grad_mlp_normed = product(grad_up_gate, weight_in, 1, 1)
    grad_residual_norm, grad_gain_two = norm_back(residual, second_gain, grad_mlp_normed)
    grad_residual = upstream + grad_residual_norm
    residual_low = grad_residual.astype(jnp.bfloat16)
    grad_attended = (
        product(weight_out, residual_low, 1, 1)
        .astype(jnp.bfloat16)
        .reshape(CHUNKS, GROUPS, HEAD_DIM, t)
    )
    total_in = reduced(product(mlp_normed, grad_up_gate, 0, 0))
    total_out = reduced(product(attended, residual_low, 1, 0))

    ups = []
    for i in range(CHUNKS):
        ups.append(exchange(grad_attended[i]))
    grad_normed = 0.0
    totals_qkv, packs, grads, parts = [], [], [], []

    def finish(query_grad, own_grad, moved):
        sums = own_grad.astype(jnp.float32)
        for grad in moved:
            sums = sums + grad.astype(jnp.float32)
        packed = jnp.stack(
            [
                unrotate(query_grad, cosine_here, sine_here),
                unrotate(sums[:, 0], cosine_here, sine_here),
                sums[:, 1],
            ],
            axis=1,
        ).astype(jnp.bfloat16)
        heads_grad = lax.dot_general(
            normed_here,
            packed.reshape(GROUPS, 3 * HEAD_DIM, t),
            (((0, 1), (0, 2)), ((), ())),
            preferred_element_type=jnp.float32,
        )
        packs.append(packed)
        grads.append(heads_grad)

    for i in range(CHUNKS):
        own, others, out, total = kept[i]
        if i > 1:
            ups[i], packs[i - 2], grads[i - 2] = lax.optimization_barrier(
                (ups[i], packs[i - 2], grads[i - 2])
            )
        query_grad, own_grad, *other_grads = attend_back(own, others, ups[i], out, total)
        moved = [across(grad, -by) for by, grad in zip(range(1, m), other_grads)]
        if i > 0:
            if i > 1:
                parts[-1], query_grad = lax.optimization_barrier((parts[-1], query_grad))
            finish(*parts[-1])
        parts.append((query_grad, own_grad, moved))
    parts[-1], grads[-1] = lax.optimization_barrier((parts[-1], grads[-1]))
    finish(*parts[-1])
    for i in range(CHUNKS):
        back = exchange(packs[i])
        totals_qkv.append(reduced_heads(grads[i]))
        back = back.transpose(1, 0, 2, 3).reshape(3 * part, t)
        grad_normed = grad_normed + product(back, weights_qkv[i], 0, 1)
    total_qkv = jnp.stack(totals_qkv).reshape(CHUNKS, GROUPS, -1, 3, HEAD_DIM)
    total_qkv = total_qkv.transpose(2, 3, 0, 1, 4).reshape(-1, 3 * width)
    grad_inputs_norm, grad_gain_one = norm_back(inputs, first_gain, grad_normed)
    tokens_grad = (grad_residual + grad_inputs_norm)[None]

    gain_rows = attn_gain.shape[0]
    gain_sums = jnp.stack([grad_gain_one, grad_gain_two])
    for axis in ("dp", "ctx"):
        bit = 1
        while bit < lax.axis_size(axis):
            gain_sums = gain_sums + swapped(gain_sums, axis, bit)
            bit *= 2
    gain_sums = lax.dynamic_slice_in_dim(gain_sums, lax.axis_index("dp") * gain_rows, gain_rows, 1)
    return (
        mixed,
        tokens_grad,
        gain_sums[0],
        gain_sums[1],
        total_qkv,
        total_out,
        total_in,
        total_down,
    )


def solution(mesh):
    return jax.shard_map(
        layer,
        mesh=mesh,
        in_specs=(
            P("dp", "ctx", None),
            P("dp", "ctx", None),
            P("dp"),
            P("dp"),
            P("dp", None),
            P("dp", None),
            P("dp", None),
            P("dp", None),
            P("dp", "ctx"),
        ),
        out_specs=(
            P("dp", "ctx", None),
            P("dp", "ctx", None),
            P("dp"),
            P("dp"),
            P("dp", None),
            P("dp", None),
            P("dp", None),
            P("dp", None),
        ),
        check_vma=False,
    )
```

```python
import functools

import jax
import jax.numpy as jnp
from jax import lax
from jax.experimental import pallas as pl
from jax.experimental.pallas import tpu as pltpu
from jax.sharding import PartitionSpec as P


HEADS = 12
HEAD_DIM = 64
FF = 1152
GROUPS = 4
CHUNKS = HEADS // GROUPS

rope_base = 160000.0
norm_eps = 1e-05


def layer_norm(values, gain):
    center = values - jnp.mean(values, axis=-1, keepdims=True)
    spread = jnp.mean(center * center, axis=-1, keepdims=True)
    return center * lax.rsqrt(spread + norm_eps) * gain


def norm_back(values, gain, upstream):
    _, pull = jax.vjp(layer_norm, values, gain)
    return pull(upstream)


def geglu(packed, hidden_size):
    return jax.nn.gelu(packed[:, :hidden_size], approximate=False) * packed[:, hidden_size:]


def product(left, right, left_dim=1, right_dim=0):
    return lax.dot_general(
        left, right, (((left_dim,), (right_dim,)), ((), ())), preferred_element_type=jnp.float32
    )


def rotate(values, cosine, sine):
    low_half, high_half = values[..., :32, :], values[..., 32:, :]
    return jnp.concatenate(
        [low_half * cosine - high_half * sine, high_half * cosine + low_half * sine], axis=-2
    )


def unrotate(values, cosine, sine):
    low_half, high_half = values[..., :32, :], values[..., 32:, :]
    return jnp.concatenate(
        [low_half * cosine + high_half * sine, high_half * cosine - low_half * sine], axis=-2
    )


def forward_kernel(m, own, *rest):
    others = rest[: m - 1]
    out, low, total, keys = rest[m - 1 :]
    n, _, d, t = own.shape
    parts = [(own, s, 1, 2) for s in range(n)] + [(r, s, 0, 1) for r in others for s in range(n)]
    for i, (ref, s, key_at, _) in enumerate(parts):
        keys[i] = ref[s, key_at].T

    def step(j, _):
        query = own[j, 0]
        top = jnp.full((1, t), -1e30, jnp.float32)
        sums = jnp.zeros((1, t), jnp.float32)
        acc = jnp.zeros((d, t), jnp.float32)
        for i, (ref, s, _, value_at) in enumerate(parts):
            scores = product(keys[i], query)
            new = jnp.maximum(top, jnp.max(scores, axis=0, keepdims=True))
            weights = jnp.exp(scores - new)
            rescale = jnp.exp(top - new)
            sums = sums * rescale + jnp.sum(weights, axis=0, keepdims=True)
            acc = acc * rescale + product(ref[s, value_at], weights.astype(jnp.bfloat16))
            top = new
        done = acc / sums
        out[j] = done
        low[j] = done.astype(jnp.bfloat16)
        total[j] = top + jnp.log(sums)
        return 0

    lax.fori_loop(0, n, step, 0)


def attend(own, others):
    n, _, d, t = own.shape
    m = 1 + len(others)
    pairs = n * t * m * n * t
    return pl.pallas_call(
        functools.partial(forward_kernel, m),
        out_shape=(
            jax.ShapeDtypeStruct((n, d, t), jnp.float32),
            jax.ShapeDtypeStruct((n, d, t), jnp.bfloat16),
            jax.ShapeDtypeStruct((n, 1, t), jnp.float32),
        ),
        scratch_shapes=[pltpu.VMEM((m * n, t, d), jnp.bfloat16)],
        cost_estimate=pl.CostEstimate(
            flops=4 * 4 * d * pairs, transcendentals=pairs, bytes_accessed=2 * 10**6
        ),
        name="attend",
    )(own, *others)


def backward_kernel(m, own, *rest):
    others = rest[: m - 1]
    upstream, out, total, query_grad, *more = rest[m - 1 :]
    grads = more[:m]
    acc, query_rows, upstream_rows, delta = more[m:]
    n, _, d, t = own.shape
    for s in range(n):
        query_rows[s] = own[s, 0].T
        upstream_rows[s] = upstream[s].T
        delta[s] = jnp.sum(upstream[s].astype(jnp.float32) * out[s], axis=0, keepdims=True)
        acc[s] = jnp.zeros((d, t), jnp.float32)
    places = [(1, 2)] + [(0, 1)] * (m - 1)
    for ref, (key_at, value_at), grad in zip((own,) + tuple(others), places, grads):

        def step(s, _):
            keys = ref[s, key_at]
            key_rows = keys.T
            value_rows = ref[s, value_at].T
            key_grad = jnp.zeros((t, d), jnp.float32)
            value_grad = jnp.zeros((t, d), jnp.float32)
            for j in range(n):
                probs = jnp.exp(product(key_rows, own[j, 0]) - total[j])
                prob_grad = product(value_rows, upstream[j])
                score_grad = (probs * (prob_grad - delta[j])).astype(jnp.bfloat16)
                value_grad = value_grad + product(probs.astype(jnp.bfloat16), upstream_rows[j])
                key_grad = key_grad + product(score_grad, query_rows[j])
                acc[j] += product(keys, score_grad)
            grad[s, 0] = key_grad.T.astype(jnp.bfloat16)
            grad[s, 1] = value_grad.T.astype(jnp.bfloat16)
            return 0

        lax.fori_loop(0, n, step, 0)
    for s in range(n):
        query_grad[s] = acc[s] * d**-0.5


def attend_back(own, others, upstream, out, total):
    n, _, d, t = own.shape
    m = 1 + len(others)
    pairs = n * t * m * n * t
    return pl.pallas_call(
        functools.partial(backward_kernel, m),
        out_shape=(jax.ShapeDtypeStruct((n, d, t), jnp.float32),)
        + tuple(jax.ShapeDtypeStruct((n, 2, d, t), jnp.bfloat16) for _ in range(m)),
        scratch_shapes=[
            pltpu.VMEM((n, d, t), jnp.float32),
            pltpu.VMEM((n, t, d), jnp.bfloat16),
            pltpu.VMEM((n, t, d), jnp.bfloat16),
            pltpu.VMEM((n, 1, t), jnp.float32),
        ],
        cost_estimate=pl.CostEstimate(
            flops=10 * 4 * d * pairs, transcendentals=pairs, bytes_accessed=4 * 10**6
        ),
        name="attend_back",
    )(own, *others, upstream, out, total)


def exchange(values):
    return lax.all_to_all(values, "ctx", 0, 0, axis_index_groups=alike())


def alike():
    count = lax.axis_size("ctx") // GROUPS
    return [[g * count + y for g in range(GROUPS)] for y in range(count)]


def across(values, by):
    count = lax.axis_size("ctx") // GROUPS
    pairs = [
        (g * count + y, g * count + (y + by) % count) for g in range(GROUPS) for y in range(count)
    ]
    return lax.ppermute(values, "ctx", pairs)


def gathered(value):
    return lax.all_gather(value, "dp", axis=0, tiled=True)


def reduced(value):
    part = lax.psum_scatter(value.astype(jnp.bfloat16), "dp", scatter_dimension=0, tiled=True)
    return lax.psum(part, "ctx").astype(jnp.float32)


def swapped(values, axis, bit):
    count = lax.axis_size(axis)
    return lax.ppermute(values, axis, [(i, i ^ bit) for i in range(count)])


def by_group(value):
    count = lax.axis_size("ctx") // GROUPS
    group = lax.axis_index("ctx") // count
    value = value[None]
    bit = 1
    while bit < GROUPS:
        other = swapped(value, "ctx", bit * count)
        value = jnp.where(
            (group // bit) % 2 == 0,
            jnp.concatenate([value, other]),
            jnp.concatenate([other, value]),
        )
        bit *= 2
    return value


def halved_over_dp(value):
    size = lax.axis_size("dp")
    place = lax.axis_index("dp")
    value = value.reshape(size, value.shape[0] // size, value.shape[1])
    bit = 1
    while bit < size:
        value = value.reshape(value.shape[0] // 2, 2, *value.shape[1:])
        mine = (place // bit) % 2
        keep = lax.dynamic_index_in_dim(value, mine, 1, keepdims=False)
        send = lax.dynamic_index_in_dim(value, 1 - mine, 1, keepdims=False)
        value = keep + swapped(send.astype(jnp.bfloat16), "dp", bit).astype(jnp.float32)
        bit *= 2
    return value[0]


def summed_over_ctx(value, count):
    bit = 1
    while bit < count:
        value = value.astype(jnp.bfloat16)
        value = value.astype(jnp.float32) + swapped(value, "ctx", bit).astype(jnp.float32)
        bit *= 2
    return value


def reduced_heads(value):
    value = summed_over_ctx(halved_over_dp(value), lax.axis_size("ctx") // GROUPS)
    return by_group(value.astype(jnp.bfloat16)).astype(jnp.float32)


def tables(positions):
    half = HEAD_DIM // 2
    frequency = rope_base ** (-jnp.arange(half, dtype=jnp.float32) / half)
    angles = frequency[:, None] * positions[..., None, :]
    return jnp.cos(angles), jnp.sin(angles)


def layer(tokens, cotangent, attn_gain, mlp_gain, w_qkv, w_out, w_in, w_mlp_out, block_offsets):
    width = HEADS * HEAD_DIM
    part = GROUPS * HEAD_DIM
    inputs = tokens[0].astype(jnp.float32)
    t = inputs.shape[0]
    m = lax.axis_size("ctx") // GROUPS
    steps = jnp.arange(t, dtype=jnp.int32)
    cosine, sine = tables((block_offsets[0, 0] + steps).astype(jnp.float32))

    gains = lax.all_gather(jnp.stack([attn_gain, mlp_gain]), "dp", axis=1, tiled=True)
    local_qkv = w_qkv.reshape(-1, 3, CHUNKS, part)
    weights_qkv = []
    for i in range(CHUNKS):
        weights_qkv.append(gathered(local_qkv[:, :, i].reshape(-1, 3 * part)))
    weight_out = gathered(w_out)
    weight_in = gathered(w_in)
    weight_down = gathered(w_mlp_out)
    offsets = by_group(block_offsets[0])
    first_gain = gains[0].astype(jnp.float32)
    second_gain = gains[1].astype(jnp.float32)

    normed = layer_norm(inputs, first_gain).astype(jnp.bfloat16)
    normed_next = normed
    kept, lows = [], []
    for i in range(CHUNKS):
        packed = product(weights_qkv[i], normed_next, 0, 1).reshape(3, GROUPS, HEAD_DIM, t)
        queries = rotate(packed[0], cosine, sine).astype(jnp.bfloat16) * HEAD_DIM**-0.5
        keys = rotate(packed[1], cosine, sine).astype(jnp.bfloat16)
        values = packed[2].astype(jnp.bfloat16)
        sent, normed_next = lax.optimization_barrier(
            (jnp.stack([queries, keys, values], axis=1), normed_next)
        )
        own = exchange(sent)
        if i == 0:
            own, offsets = lax.optimization_barrier((own, offsets))
        others = [across(own[:, 1:], by) for by in range(1, m)]
        out, low, total = attend(own, others)
        lows.append(exchange(low).reshape(part, t))
        kept.append((own, others, out, total))
    attended = jnp.concatenate(lows, axis=0)
    normed_here = lax.all_gather(normed, "ctx", axis=0, axis_index_groups=alike())
    cosine_here, sine_here = tables((offsets + steps).astype(jnp.float32))

    residual = inputs + product(attended, weight_out, 0, 0)
    mlp_normed = layer_norm(residual, second_gain).astype(jnp.bfloat16)
    up_gate = product(mlp_normed, weight_in)
    joined = geglu(up_gate, FF).astype(jnp.bfloat16)
    mixed = (residual + product(joined, weight_down)).astype(jnp.bfloat16)[None]

    upstream_low = cotangent[0]
    upstream = upstream_low.astype(jnp.float32)
    grad_down = product(joined, upstream_low, 0, 0).astype(jnp.bfloat16)
    upstream_low, grad_down = lax.optimization_barrier((upstream_low, grad_down))
    total_down = reduced(grad_down)
    grad_joined = product(upstream_low, weight_down, 1, 1)
    _, glu_pull = jax.vjp(lambda packed_in: geglu(packed_in, FF), up_gate)
    grad_up_gate = glu_pull(grad_joined)[0].astype(jnp.bfloat16)
    grad_mlp_normed = product(grad_up_gate, weight_in, 1, 1)
    grad_residual_norm, grad_gain_two = norm_back(residual, second_gain, grad_mlp_normed)
    grad_residual = upstream + grad_residual_norm
    residual_low = grad_residual.astype(jnp.bfloat16)
    grad_attended = (
        product(weight_out, residual_low, 1, 1)
        .astype(jnp.bfloat16)
        .reshape(CHUNKS, GROUPS, HEAD_DIM, t)
    )
    total_in = reduced(product(mlp_normed, grad_up_gate, 0, 0))
    total_out = summed_over_ctx(
        halved_over_dp(product(attended, residual_low, 1, 0)), lax.axis_size("ctx")
    )

    ups = [exchange(grad_attended[0])]
    later = exchange(grad_attended[1:].transpose(1, 0, 2, 3))
    ups += [later[:, i] for i in range(CHUNKS - 1)]
    grad_normed = 0.0
    totals_qkv, packs, grads, parts = [], [], [], []

    def finish(query_grad, own_grad, moved):
        sums = own_grad.astype(jnp.float32)
        for grad in moved:
            sums = sums + grad.astype(jnp.float32)
        packed = jnp.stack(
            [
                unrotate(query_grad, cosine_here, sine_here),
                unrotate(sums[:, 0], cosine_here, sine_here),
                sums[:, 1],
            ],
            axis=1,
        ).astype(jnp.bfloat16)
        heads_grad = lax.dot_general(
            normed_here,
            packed.reshape(GROUPS, 3 * HEAD_DIM, t),
            (((0, 1), (0, 2)), ((), ())),
            preferred_element_type=jnp.float32,
        )
        packs.append(packed)
        grads.append(heads_grad)

    for i in range(CHUNKS):
        own, others, out, total = kept[i]
        if i > 1:
            ups[i], packs[i - 2], grads[i - 2] = lax.optimization_barrier(
                (ups[i], packs[i - 2], grads[i - 2])
            )
        query_grad, own_grad, *other_grads = attend_back(own, others, ups[i], out, total)
        moved = [across(grad, -by) for by, grad in zip(range(1, m), other_grads)]
        if i > 0:
            if i > 1:
                parts[-1], query_grad = lax.optimization_barrier((parts[-1], query_grad))
            finish(*parts[-1])
        parts.append((query_grad, own_grad, moved))
    parts[-1], grads[-1] = lax.optimization_barrier((parts[-1], grads[-1]))
    finish(*parts[-1])
    for i in range(CHUNKS):
        back = exchange(packs[i])
        totals_qkv.append(reduced_heads(grads[i]))
        back = back.transpose(1, 0, 2, 3).reshape(3 * part, t)
        grad_normed = grad_normed + product(back, weights_qkv[i], 0, 1)
    total_qkv = jnp.stack(totals_qkv).reshape(CHUNKS, GROUPS, -1, 3, HEAD_DIM)
    total_qkv = total_qkv.transpose(2, 3, 0, 1, 4).reshape(-1, 3 * width)
    grad_inputs_norm, grad_gain_one = norm_back(inputs, first_gain, grad_normed)
    tokens_grad = (grad_residual + grad_inputs_norm)[None]

    gain_rows = attn_gain.shape[0]
    gain_sums = jnp.stack([grad_gain_one, grad_gain_two])
    for axis in ("dp", "ctx"):
        bit = 1
        while bit < lax.axis_size(axis):
            gain_sums = gain_sums + swapped(gain_sums, axis, bit)
            bit *= 2
    gain_sums = lax.dynamic_slice_in_dim(gain_sums, lax.axis_index("dp") * gain_rows, gain_rows, 1)
    return (
        mixed,
        tokens_grad,
        gain_sums[0],
        gain_sums[1],
        total_qkv,
        total_out,
        total_in,
        total_down,
    )


def solution(mesh):
    return jax.shard_map(
        layer,
        mesh=mesh,
        in_specs=(
            P("dp", "ctx", None),
            P("dp", "ctx", None),
            P("dp"),
            P("dp"),
            P("dp", None),
            P("dp", None),
            P("dp", None),
            P("dp", None),
            P("dp", "ctx"),
        ),
        out_specs=(
            P("dp", "ctx", None),
            P("dp", "ctx", None),
            P("dp"),
            P("dp"),
            P("dp", None),
            P("dp", None),
            P("dp", None),
            P("dp", None),
        ),
        check_vma=False,
    )
```
